32 devices in a mesh: ctx: 8 (over z, x), head: 2 (over y), dp: 2 (over core).
Axes of the slice: x: 2, y: 2, z: 4, core: 2. Of those that a mesh axis runs over, the one named last changes fastest.
Arguments:
- queries: bfloat16 [2, 2048, 32, 128], P('dp', 'ctx', 'head'), may hold values from -7 to 7
- keys: bfloat16 [2, 2048, 16, 128], P('dp', 'ctx', 'head'), may hold values from -7 to 7
- values: bfloat16 [2, 2048, 16, 128], P('dp', 'ctx', 'head'), may hold values from -6 to 6
- d_out: bfloat16 [2, 2048, 32, 128], P('dp', 'ctx', 'head'), may hold values from -6 to 6
- loss_mask: int32 [2, 2048], P('dp', 'ctx'), may hold values from 0 to 1, as said below
- turn_ids: int32 [2, 2048], P('dp', 'ctx'), may hold values from 0 to 1, never falling along the last dimension, each value on 1 to 1536 neighbouring positions
Outputs:
- d_queries: bfloat16 [2, 2048, 32, 128], P('dp', 'ctx', 'head')
- d_keys: bfloat16 [2, 2048, 16, 128], P('dp', 'ctx', 'head')
- d_values: bfloat16 [2, 2048, 16, 128], P('dp', 'ctx', 'head')
The draws below stay inside these ranges and needn't reach their ends.
Inputs may be any that keep to these rules, and one draw needn't show every extreme that they name: `loss_mask`: within each trajectory the share of ones grows with the position; position 0 of every trajectory is 1. `turn_ids`: turn ids never fall along a trajectory; each turn holds 1 to 1536 positions.
All inputs are finite; a program needn't handle non-finite values.
Results may differ from the reference program's by a relative error of at most 0.015.
Values may be sent and summed in bfloat16 or wider, within the bound.
A program may use at most 128 MiB of HBM per device.

```python
import math
import jax
import jax.numpy as jnp
import numpy as np
from jax import lax

QH = 32
KVH = 16
DH = 128
WINDOW = 1024
TOK_DEV = 256
TRAJ = 2
SEQ = 2048
TURNS = 2


def draw_loss_mask(key, part):
    span_count = SEQ // 8
    draw_values = jax.random.randint(jax.random.fold_in(key, 11), (TRAJ, span_count), 0, 5 * SEQ)
    span_start = jnp.arange(span_count, dtype=jnp.int32) * 8
    kept = (draw_values < SEQ + 3 * span_start[None, :]).astype(jnp.int32)
    mask_full = jnp.repeat(kept, 8, axis=1)
    return mask_full.at[:, 0].set(1)


def attention_pair(key):
    base_key = jax.random.fold_in(key, 23)
    subkeys = jax.random.split(base_key, 2)
    query_shape = (TRAJ, SEQ, QH, DH)
    key_shape = (TRAJ, SEQ, KVH, DH)
    query_new = jnp.clip(jax.random.normal(subkeys[0], query_shape, jnp.float32), -6.0, 6.0)
    key_new = jnp.clip(jax.random.normal(subkeys[1], key_shape, jnp.float32), -6.0, 6.0)
    return (query_new.astype(jnp.bfloat16), key_new.astype(jnp.bfloat16))


def draw_queries(key, part):
    return attention_pair(key)[0]


def draw_keys(key, part):
    return attention_pair(key)[1]


def block_scale(stream_key, shape, cuts, low, high):
    def one(axis_at, parts):
        heights = jax.random.uniform(jax.random.fold_in(jax.random.fold_in(stream_key, 6), axis_at), (parts,), jnp.float32, low / len(cuts), high / len(cuts))
        return jnp.repeat(jnp.exp(heights), shape[axis_at] // parts).reshape((-1,) + (1,) * (len(shape) - axis_at - 1))

    level = one(*cuts[0])
    for cut in cuts[1:]:
        level = level * one(*cut)
    return level


def profile(count, total, most, lean):
    loads = [(1 << 20) // math.isqrt(rank ** lean) + 1 for rank in range(2, count + 1)]
    spare, counts = total - most - (count - 1), [1] * (count - 1)
    while spare > 0:
        free = [i for i in range(count - 1) if counts[i] < most]
        whole, budget = sum([loads[i] for i in free]), spare
        for i in free:
            more = min(most - counts[i], max(1, budget * loads[i] // whole), spare)
            counts[i] = counts[i] + more
            spare = spare - more
    return np.array([most] + counts)


def ragged_sizes(stream_key, number_of, total, reach, lean):
    if number_of == 2:
        one = jax.random.randint(stream_key, (), max(1, total - reach), min(reach, total - 1) + 1)
        return jnp.stack([one, total - one])
    tallies = jnp.asarray(profile(number_of, total, reach, lean), jnp.int32)
    twos = (number_of - 1) // 2
    donor, taker = tallies[1:1 + 2 * twos:2], tallies[2:2 + 2 * twos:2]
    slack = jnp.minimum(donor - 1, reach - taker)
    passed = jax.random.randint(jax.random.fold_in(stream_key, 1), (twos,), 0, 1 << 20) % (slack + 1)
    tallies = tallies.at[1:1 + 2 * twos:2].set(donor - passed).at[2:2 + 2 * twos:2].set(taker + passed)
    return tallies[jax.random.permutation(jax.random.fold_in(stream_key, 2), number_of)]


def bell_draw(rng, shape, scale, bound, shards=(), kind=jnp.bfloat16):
    level = block_scale(rng, shape, shards, -0.22, 0.18) if shards else 1.0
    values = jax.random.normal(rng, shape, jnp.float32) * scale * level
    return jnp.minimum(jnp.maximum(values, -bound), bound).astype(kind)


def setup_inputs(seed: int = 0) -> dict:
    streams_of = jax.random.split(jax.random.key(seed), 7)
    return {
        "queries": draw_queries(jax.random.fold_in(streams_of[6], 71), 0),
        "keys": draw_keys(jax.random.fold_in(streams_of[6], 71), 0),
        "values": bell_draw(streams_of[2], (TRAJ, SEQ, KVH, DH), 1.0, 6.0, ((0, 2), (1, 8), (2, 2))),
        "d_out": bell_draw(streams_of[3], (TRAJ, SEQ, QH, DH), 1.0, 6.0, ((0, 2), (1, 8), (2, 2))),
        "loss_mask": draw_loss_mask(jax.random.fold_in(streams_of[6], 71), 0),
        "turn_ids": jax.vmap(lambda own: jnp.searchsorted(jnp.cumsum(ragged_sizes(own, TURNS, SEQ, 6 * TOK_DEV, 0)), jnp.arange(SEQ), side="right"))(jax.random.split(streams_of[5], TRAJ)).reshape((TRAJ, SEQ)).astype(jnp.int32),
    }


SCALE = 168.0 ** -0.5


def round_keep(array):
    return lax.optimization_barrier(array.astype(jnp.bfloat16)).astype(jnp.float32)


def reference(queries, keys, values, d_out, loss_mask, turn_ids):
    count_all = jnp.sum(loss_mask).astype(jnp.float32)
    factor = (TRAJ * SEQ) / count_all
    group_size = QH // KVH
    key_span = WINDOW + TOK_DEV
    row_index = lax.broadcasted_iota(jnp.int32, (TOK_DEV, key_span), 0)
    col_index = lax.broadcasted_iota(jnp.int32, (TOK_DEV, key_span), 1)
    query_list = []
    key_list = []
    value_list = []
    for member in range(TRAJ):
        query_all = queries[member].astype(jnp.float32).reshape(SEQ, KVH, group_size, DH)
        weighted = d_out[member] * loss_mask[member][:, None, None].astype(jnp.bfloat16)
        grad_all = weighted.astype(jnp.float32).reshape(SEQ, KVH, group_size, DH)
        pad_keys = jnp.concatenate([jnp.zeros((WINDOW, KVH, DH), jnp.float32), keys[member].astype(jnp.float32)], 0)
        pad_values = jnp.concatenate([jnp.zeros((WINDOW, KVH, DH), jnp.float32), values[member].astype(jnp.float32)], 0)
        turn_marks = (turn_ids[member] + 1).astype(jnp.int32)
        pad_marks = jnp.concatenate([jnp.zeros((WINDOW,), jnp.int32), turn_marks], 0)

        def block_step(running, block_index):
            key_acc, value_acc = running
            offset = (block_index * TOK_DEV).astype(jnp.int32)
            query_block = lax.dynamic_slice_in_dim(query_all, offset, TOK_DEV, 0)
            grad_block = lax.dynamic_slice_in_dim(grad_all, offset, TOK_DEV, 0)
            key_block = lax.dynamic_slice_in_dim(pad_keys, offset, key_span, 0)
            value_block = lax.dynamic_slice_in_dim(pad_values, offset, key_span, 0)
            mark_query = lax.dynamic_slice_in_dim(turn_marks, offset, TOK_DEV, 0)
            mark_key = lax.dynamic_slice_in_dim(pad_marks, offset, key_span, 0)
            allowed = (col_index > row_index) & (col_index <= row_index + WINDOW) & (mark_key[None, :] == mark_query[:, None])
            logits = jnp.einsum("tkgd,jkd->kgtj", query_block, key_block) * SCALE
            logits = jnp.where(allowed, logits, -jnp.inf)
            top_score = jnp.max(logits, axis=3, keepdims=True)
            raised = jnp.exp(logits - top_score)
            totals = jnp.sum(raised, axis=3, keepdims=True)
            prob_f32 = raised / totals
            prob_round = round_keep(prob_f32)
            outputs = round_keep(jnp.einsum("kgtj,jkd->tkgd", prob_round, value_block))
            deltas = jnp.sum(grad_block * outputs, axis=3)
            grad_probs = jnp.einsum("tkgd,jkd->kgtj", grad_block, value_block)
            grad_logits = prob_f32 * (grad_probs - jnp.transpose(deltas, (1, 2, 0))[..., None]) * SCALE
            grad_round = round_keep(grad_logits)
            grad_query = jnp.einsum("kgtj,jkd->tkgd", grad_round, key_block)
            grad_key = jnp.einsum("kgtj,tkgd->jkd", grad_round, query_block)
            grad_value = jnp.einsum("kgtj,tkgd->jkd", prob_round, grad_block)
            key_acc = lax.dynamic_update_slice_in_dim(key_acc, lax.dynamic_slice_in_dim(key_acc, offset, key_span, 0) + grad_key, offset, 0)
            value_acc = lax.dynamic_update_slice_in_dim(value_acc, lax.dynamic_slice_in_dim(value_acc, offset, key_span, 0) + grad_value, offset, 0)
            return (key_acc, value_acc), grad_query

        start_acc = jnp.zeros((WINDOW + SEQ, KVH, DH), jnp.float32)
        finals, grad_query = lax.scan(block_step, (start_acc, start_acc), jnp.arange(SEQ // TOK_DEV, dtype=jnp.int32))
        query_list.append((grad_query.reshape(SEQ, QH, DH) * factor).astype(jnp.bfloat16))
        key_list.append((finals[0][WINDOW:] * factor).astype(jnp.bfloat16))
        value_list.append((finals[1][WINDOW:] * factor).astype(jnp.bfloat16))
    return jnp.stack(query_list), jnp.stack(key_list), jnp.stack(value_list)
```

```python
import functools
import math

import jax
import jax.numpy as jnp
from jax import lax
from jax.experimental import pallas as pl
from jax.experimental.pallas import tpu as pltpu
from jax.sharding import PartitionSpec as P

WINDOW = 1024
SCALE = 168.0 ** (-0.5)
STRIP = 128
MASKED = -1e30


def head_grads(head, rows, q_ref, g_ref, ext, bias, acc, dq_ref):
    span = WINDOW + STRIP
    for strip in range(rows // STRIP):
        low = strip * STRIP
        query = q_ref[head, strip]
        grad = g_ref[head, strip]
        key = ext[head, 0, low : low + span, :]
        value = ext[head, 1, low : low + span, :]
        logits = lax.dot_general(
            key, query, (((1,), (1,)), ((), ())), preferred_element_type=jnp.float32
        )
        logits = logits * (SCALE * math.log2(math.e)) + bias[strip]
        top = jnp.max(logits, axis=0, keepdims=True)
        raised = jnp.exp2(logits - top)
        prob = raised * (1.0 / jnp.sum(raised, axis=0, keepdims=True))
        grad_prob = lax.dot_general(
            value, grad, (((1,), (1,)), ((), ())), preferred_element_type=jnp.float32
        )
        delta = jnp.sum(prob * grad_prob, axis=0, keepdims=True)
        grad_logit = (prob * (grad_prob - delta)).astype(jnp.bfloat16)
        dq_ref[head, strip] = lax.dot_general(
            grad_logit, key, (((0,), (0,)), ((), ())), preferred_element_type=jnp.float32
        )
        parts = (
            jnp.dot(grad_logit, query, preferred_element_type=jnp.float32),
            jnp.dot(prob.astype(jnp.bfloat16), grad, preferred_element_type=jnp.float32),
        )
        for kind, part in enumerate(parts):
            if strip == 0:
                acc[kind, :span] = part
            else:
                cut = span - STRIP
                acc[kind, low : low + cut] += part[:cut]
                acc[kind, low + cut : low + span] = part[cut:]


def fill_bias(rows, mark_ref, low_ref, marks, bias):
    hops = WINDOW // rows
    first = mark_ref[0:1, 0:1]
    before = jnp.zeros((1, 1), jnp.float32)
    for hop in range(hops):
        earlier = jnp.where(marks[hop, 0:1, :] < first, 1.0, 0.0)
        before += jnp.sum(earlier, axis=1, keepdims=True)
    for strip in range(rows // STRIP):
        own = low_ref[strip, 0:1, :].astype(jnp.float32)
        start = jnp.where(own > 0.0, own + WINDOW, before) - strip * STRIP
        shape = bias.shape[1:]
        row = lax.broadcasted_iota(jnp.int32, (1, shape[1]), 1) & (STRIP - 1)
        lowest = jnp.maximum(start.astype(jnp.int32), row + 1)
        col = lax.broadcasted_iota(jnp.int32, shape, 0)
        ok = (col >= lowest) & (col <= row + WINDOW)
        bias[strip] = jnp.where(ok, 0.0, MASKED)


def kernel(
    n, rows, q_ref, g_ref, kv_ref, mark_ref, low_ref, dq_ref, dkv_ref,
    ext, sent, back, marks, bias, acc,
    mark_send, mark_recv, kv_send, kv_recv, back_send, back_recv,
):
    hops = WINDOW // rows
    heads = kv_ref.shape[0]
    me = lax.axis_index("ctx")

    def mark_copy(d):
        return pltpu.make_async_remote_copy(
            src_ref=mark_ref, dst_ref=marks.at[d - 1],
            send_sem=mark_send.at[d - 1], recv_sem=mark_recv.at[d - 1],
            device_id={"ctx": me + d}, device_id_type=pl.DeviceIdType.MESH,
        )

    def kv_copy(head, d):
        return pltpu.make_async_remote_copy(
            src_ref=kv_ref.at[head],
            dst_ref=ext.at[head, :, pl.ds(WINDOW - d * rows, rows), :],
            send_sem=kv_send.at[head, d - 1], recv_sem=kv_recv.at[head, d - 1],
            device_id={"ctx": me + d}, device_id_type=pl.DeviceIdType.MESH,
        )

    def back_copy(head, d):
        return pltpu.make_async_remote_copy(
            src_ref=sent.at[head, d - 1], dst_ref=back.at[head, d - 1],
            send_sem=back_send.at[head, d - 1], recv_sem=back_recv.at[head, d - 1],
            device_id={"ctx": me - d}, device_id_type=pl.DeviceIdType.MESH,
        )

    barrier = pltpu.get_barrier_semaphore()
    for d in range(1, hops + 1):
        @pl.when(me + d < n)
        def _():
            pl.semaphore_signal(barrier, inc=1, device_id={"ctx": me + d},
                                device_id_type=pl.DeviceIdType.MESH)

        @pl.when(me >= d)
        def _():
            pl.semaphore_signal(barrier, inc=1, device_id={"ctx": me - d},
                                device_id_type=pl.DeviceIdType.MESH)
    pl.semaphore_wait(barrier, jnp.minimum(me, hops) + jnp.minimum(n - 1 - me, hops))

    for d in range(1, hops + 1):
        @pl.when(me + d < n)
        def _():
            mark_copy(d).start()

    def send_head(head, carry):
        for d in range(1, hops + 1):
            @pl.when(me + d < n)
            def _():
                kv_copy(head, d).start()
        ext[head, :, WINDOW : WINDOW + rows, :] = kv_ref[head]
        for d in range(1, hops + 1):
            @pl.when(me < d)
            def _():
                ext[head, :, WINDOW - d * rows : WINDOW - (d - 1) * rows, :] = jnp.zeros(
                    (2, rows, kv_ref.shape[3]), kv_ref.dtype
                )
        return carry

    lax.fori_loop(0, heads, send_head, 0)

    for d in range(1, hops + 1):
        @pl.when(me < d)
        def _():
            marks[d - 1] = jnp.full(mark_ref.shape, -1, jnp.int32)

        @pl.when(me >= d)
        def _():
            mark_copy(d).wait_recv()
    fill_bias(rows, mark_ref, low_ref, marks, bias)

    def do_head(head, carry):
        for d in range(1, hops + 1):
            @pl.when(me >= d)
            def _():
                kv_copy(head, d).wait_recv()
        head_grads(head, rows, q_ref, g_ref, ext, bias, acc, dq_ref)
        for d in range(1, hops + 1):
            low = WINDOW - d * rows
            sent[head, d - 1] = acc[:, low : low + rows, :].astype(sent.dtype)

            @pl.when(me >= d)
            def _():
                back_copy(head, d).start()
        dkv_ref[head] = acc[:, WINDOW : WINDOW + rows, :]
        return carry

    lax.fori_loop(0, heads, do_head, 0)

    def finish_head(head, carry):
        for d in range(1, hops + 1):
            @pl.when(me + d < n)
            def _():
                back_copy(head, d).wait_recv()
                dkv_ref[head] += back[head, d - 1].astype(jnp.float32)
        for d in range(1, hops + 1):
            @pl.when(me + d < n)
            def _():
                kv_copy(head, d).wait_send()

            @pl.when(me >= d)
            def _():
                back_copy(head, d).wait_send()
        return carry

    lax.fori_loop(0, heads, finish_head, 0)
    for d in range(1, hops + 1):
        @pl.when(me + d < n)
        def _():
            mark_copy(d).wait_send()


def on_device(queries, keys, values, d_out, loss_mask, turn_ids):
    rows, heads_q, depth = queries.shape[1:]
    heads = keys.shape[2]
    group = heads_q // heads
    n = lax.axis_size("ctx")
    hops = WINDOW // rows
    strips = rows // STRIP
    wide = group * STRIP
    count_all = lax.psum(jnp.sum(loss_mask).astype(jnp.float32), ("ctx", "dp"))
    factor = rows * n * lax.axis_size("dp") / count_all

    def by_strip(array):
        array = array.reshape(strips, STRIP, heads, group, depth)
        return array.transpose(2, 0, 3, 1, 4).reshape(heads, strips, wide, depth)

    q = by_strip(queries[0])
    g = by_strip(d_out[0] * loss_mask[0][:, None, None].astype(jnp.bfloat16))
    kv = jnp.stack([keys[0], values[0]]).transpose(2, 0, 1, 3)
    turn = turn_ids[0]
    own_low = jnp.sum((turn[None, :] < turn[:, None]).astype(jnp.int32), axis=1)
    own_low = own_low.reshape(strips, 1, 1, STRIP)
    own_low = jnp.broadcast_to(own_low, (strips, 8, group, STRIP)).reshape(strips, 8, wide)
    mark = jnp.broadcast_to(turn[None, :], (8, rows))
    vmem = pl.BlockSpec(memory_space=pltpu.VMEM)
    span = WINDOW + rows
    dq, dkv = pl.pallas_call(
        functools.partial(kernel, n, rows),
        out_shape=(
            jax.ShapeDtypeStruct((heads, strips, wide, depth), jnp.float32),
            jax.ShapeDtypeStruct((heads, 2, rows, depth), jnp.float32),
        ),
        in_specs=[vmem] * 5,
        out_specs=(vmem, vmem),
        scratch_shapes=[
            pltpu.VMEM((heads, 2, span, depth), jnp.bfloat16),
            pltpu.VMEM((heads, hops, 2, rows, depth), jnp.bfloat16),
            pltpu.VMEM((heads, hops, 2, rows, depth), jnp.bfloat16),
            pltpu.VMEM((hops, 8, rows), jnp.int32),
            pltpu.VMEM((strips, WINDOW + STRIP, wide), jnp.float32),
            pltpu.VMEM((2, span, depth), jnp.float32),
            pltpu.SemaphoreType.DMA((hops,)),
            pltpu.SemaphoreType.DMA((hops,)),
            pltpu.SemaphoreType.DMA((heads, hops)),
            pltpu.SemaphoreType.DMA((heads, hops)),
            pltpu.SemaphoreType.DMA((heads, hops)),
            pltpu.SemaphoreType.DMA((heads, hops)),
        ],
        compiler_params=pltpu.CompilerParams(
            collective_id=0, has_side_effects=True, vmem_limit_bytes=56 << 20
        ),
    )(q, g, kv, mark, own_low)
    d_q = (dq * (factor * SCALE)).astype(jnp.bfloat16)
    d_q = d_q.reshape(heads, strips, group, STRIP, depth).transpose(1, 3, 0, 2, 4)
    d_queries = d_q.reshape(1, rows, heads_q, depth)
    d_keys = (dkv[:, 0] * (factor * SCALE)).astype(jnp.bfloat16).transpose(1, 0, 2)[None]
    d_values = (dkv[:, 1] * factor).astype(jnp.bfloat16).transpose(1, 0, 2)[None]
    return (d_queries, d_keys, d_values)


def solution(mesh):
    spec = P("dp", "ctx", "head", None)
    return jax.shard_map(
        on_device,
        mesh=mesh,
        in_specs=(spec, spec, spec, spec, P("dp", "ctx"), P("dp", "ctx")),
        out_specs=(spec, spec, spec),
        check_vma=False,
    )
```

```python
import functools
import math

import jax
import jax.numpy as jnp
from jax import lax
from jax.experimental import pallas as pl
from jax.experimental.pallas import tpu as pltpu
from jax.sharding import PartitionSpec as P

WINDOW = 1024
SCALE = 168.0 ** (-0.5)
STRIP = 128
MASKED = -1e30
AHEAD = 2


def head_grads(head, rows, q_ref, g_ref, ext, bias, acc, dq_ref):
    span = WINDOW + STRIP
    for strip in range(rows // STRIP):
        low = strip * STRIP
        query = q_ref[head, strip]
        grad = g_ref[head, strip]
        key = ext[head, 0, low : low + span, :]
        value = ext[head, 1, low : low + span, :]
        logits = lax.dot_general(
            key, query, (((1,), (1,)), ((), ())), preferred_element_type=jnp.float32
        )
        logits = logits * (SCALE * math.log2(math.e)) + bias[strip]
        top = jnp.max(logits, axis=0, keepdims=True)
        raised = jnp.exp2(logits - top)
        prob = raised * (1.0 / jnp.sum(raised, axis=0, keepdims=True))
        grad_prob = lax.dot_general(
            value, grad, (((1,), (1,)), ((), ())), preferred_element_type=jnp.float32
        )
        delta = jnp.sum(prob * grad_prob, axis=0, keepdims=True)
        grad_logit = (prob * (grad_prob - delta)).astype(jnp.bfloat16)
        dq_ref[head, strip] = lax.dot_general(
            grad_logit, key, (((0,), (0,)), ((), ())), preferred_element_type=jnp.float32
        )
        parts = (
            jnp.dot(grad_logit, query, preferred_element_type=jnp.float32),
            jnp.dot(prob.astype(jnp.bfloat16), grad, preferred_element_type=jnp.float32),
        )
        for kind, part in enumerate(parts):
            if strip == 0:
                acc[kind, :span] = part
            else:
                cut = span - STRIP
                acc[kind, low : low + cut] += part[:cut]
                acc[kind, low + cut : low + span] = part[cut:]


def fill_bias(rows, mark_ref, low_ref, marks, bias):
    hops = WINDOW // rows
    first = mark_ref[0:1, 0:1]
    before = jnp.zeros((1, 1), jnp.float32)
    for hop in range(hops):
        earlier = jnp.where(marks[hop, 0:1, :] < first, 1.0, 0.0)
        before += jnp.sum(earlier, axis=1, keepdims=True)
    for strip in range(rows // STRIP):
        own = low_ref[strip, 0:1, :].astype(jnp.float32)
        start = jnp.where(own > 0.0, own + WINDOW, before) - strip * STRIP
        shape = bias.shape[1:]
        row = lax.broadcasted_iota(jnp.int32, (1, shape[1]), 1) & (STRIP - 1)
        lowest = jnp.maximum(start.astype(jnp.int32), row + 1)
        col = lax.broadcasted_iota(jnp.int32, shape, 0)
        ok = (col >= lowest) & (col <= row + WINDOW)
        bias[strip] = jnp.where(ok, 0.0, MASKED)


def kernel(
    n, pairs, rows, q_ref, g_ref, kv_ref, mark_ref, low_ref, count_ref,
    dq_ref, dkv_ref, total_ref,
    ext, sent, back, marks, bias, acc, count, count_in,
    mark_send, mark_recv, kv_send, kv_recv, back_send, back_recv, count_send, count_recv,
):
    hops = WINDOW // rows
    heads = kv_ref.shape[0]
    me = lax.axis_index("ctx")
    odd = me % 2
    other = me + 1 - 2 * odd
    bits = [("ctx", 1 << b) for b in range(n.bit_length() - 1)]
    bits += [("dp", 1 << b) for b in range(pairs.bit_length() - 1)]

    def remote(src, dst, send, recv, device):
        return pltpu.make_async_remote_copy(
            src_ref=src, dst_ref=dst, send_sem=send, recv_sem=recv,
            device_id=device, device_id_type=pl.DeviceIdType.MESH,
        )

    def partner(axis, bit):
        at = lax.axis_index(axis)
        return {axis: at + bit - 2 * bit * ((at // bit) % 2)}

    def mark_copy(d):
        return remote(mark_ref, marks.at[d - 1], mark_send.at[d - 1], mark_recv.at[d - 1],
                      {"ctx": me + d})

    def count_copy(k):
        return remote(count.at[k], count_in.at[k], count_send.at[k], count_recv.at[k],
                      partner(*bits[k]))

    def slot(head, d):
        return ext.at[head, :, pl.ds(WINDOW - d * rows, rows), :]

    def kv_copy(head, d):
        if d == 1:
            return remote(slot(head, 2), slot(head, 1), kv_send.at[head, 0],
                          kv_recv.at[head, 0], {"ctx": other})
        src = kv_ref.at[head] if d == 2 else slot(head, d - 2)
        return remote(src, slot(head, d), kv_send.at[head, d - 1], kv_recv.at[head, d - 1],
                      {"ctx": me + 2})

    def own_across(head):
        return remote(kv_ref.at[head], slot(head, 1), kv_send.at[head, 0],
                      kv_recv.at[head, 0], {"ctx": other})

    def back_copy(head, d):
        return remote(sent.at[head, d - 1], back.at[head, d - 1], back_send.at[head, d - 1],
                      back_recv.at[head, d - 1], {"ctx": other if d == 1 else me - 2})

    def add_in(head, d, taken):
        sent[head, d - 1] = (
            sent[head, d - 1].astype(jnp.float32) + back[head, taken - 1].astype(jnp.float32)
        ).astype(sent.dtype)

    barrier = pltpu.get_barrier_semaphore()

    def greet(device):
        pl.semaphore_signal(barrier, inc=1, device_id=device,
                            device_id_type=pl.DeviceIdType.MESH)

    for d in range(1, hops + 1):
        @pl.when(me + d < n)
        def _():
            greet({"ctx": me + d})

        @pl.when(me >= d)
        def _():
            greet({"ctx": me - d})
    far = [b for b in bits if b[0] == "dp" or b[1] > hops]
    for b in far:
        greet(partner(*b))
    pl.semaphore_wait(
        barrier, jnp.minimum(me, hops) + jnp.minimum(n - 1 - me, hops) + len(far)
    )

    def send_own(head):
        @pl.when(me + 2 < n)
        def _():
            kv_copy(head, 2).start()

        @pl.when(odd == 0)
        def _():
            own_across(head).start()

    for d in range(1, hops + 1):
        @pl.when(me + d < n)
        def _():
            mark_copy(d).start()
    for head in range(min(AHEAD, heads)):
        send_own(head)
    count[0] = count_ref[...]
    count_copy(0).start()

    def place_own(head, carry):
        ext[head, :, WINDOW : WINDOW + rows, :] = kv_ref[head]
        for d in range(1, hops + 1):
            @pl.when(me < d)
            def _():
                ext[head, :, WINDOW - d * rows : WINDOW - (d - 1) * rows, :] = jnp.zeros(
                    (2, rows, kv_ref.shape[3]), kv_ref.dtype
                )
        return carry

    lax.fori_loop(0, heads, place_own, 0)

    for d in range(1, hops + 1):
        @pl.when(me < d)
        def _():
            marks[d - 1] = jnp.full(mark_ref.shape, -1, jnp.int32)

        @pl.when(me >= d)
        def _():
            mark_copy(d).wait_recv()
    fill_bias(rows, mark_ref, low_ref, marks, bias)

    def step(s, carry):
        for k in range(len(bits)):
            @pl.when(s == k)
            def _():
                count_copy(k).wait_recv()
                count[k + 1] = count[k] + count_in[k]
                if k + 1 < len(bits):
                    count_copy(k + 1).start()

        @pl.when(s + AHEAD < heads)
        def _():
            send_own(s + AHEAD)

        @pl.when(s < heads)
        def _():
            @pl.when(me >= 2)
            def _():
                kv_copy(s, 2).wait_recv()

                @pl.when(odd == 1)
                def _():
                    kv_copy(s, 1).start()

                @pl.when(me + 2 < n)
                def _():
                    kv_copy(s, 4).start()

            @pl.when(odd == 1)
            def _():
                kv_copy(s, 1).wait_recv()

                @pl.when(me + 2 < n)
                def _():
                    kv_copy(s, 3).start()

        @pl.when((s >= 1) & (s < heads + 1) & (odd == 0) & (me >= 2))
        def _():
            kv_copy(s - 1, 1).wait_recv()

            @pl.when(me + 2 < n)
            def _():
                kv_copy(s - 1, 3).start()

        @pl.when((s >= 3) & (s < heads + 3))
        def _():
            head = s - 3

            @pl.when(me >= 1)
            def _():
                @pl.when(me + 2 < n)
                def _():
                    back_copy(head, 3).wait_recv()
                    add_in(head, 1, 3)

                back_copy(head, 1).start()

            @pl.when((odd == 0) & (me >= 2))
            def _():
                @pl.when(me + 2 < n)
                def _():
                    back_copy(head, 4).wait_recv()
                    add_in(head, 2, 4)

                back_copy(head, 2).start()

        @pl.when((s >= 4) & (s < heads + 4) & (odd == 1) & (me >= 2))
        def _():
            head = s - 4

            @pl.when(me + 2 < n)
            def _():
                back_copy(head, 4).wait_recv()
                add_in(head, 2, 4)

            back_copy(head, 1).wait_recv()
            add_in(head, 2, 1)
            back_copy(head, 2).start()

        @pl.when(s >= 5)
        def _():
            head = s - 5

            @pl.when(odd == 0)
            def _():
                back_copy(head, 1).wait_recv()
                dkv_ref[head] += back[head, 0].astype(jnp.float32)

            @pl.when(me + 2 < n)
            def _():
                back_copy(head, 2).wait_recv()
                dkv_ref[head] += back[head, 1].astype(jnp.float32)

        @pl.when((s >= 2) & (s < heads + 2))
        def _():
            head = s - 2
            for d in (3, 4):
                @pl.when(me >= d)
                def _():
                    kv_copy(head, d).wait_recv()
            head_grads(head, rows, q_ref, g_ref, ext, bias, acc, dq_ref)
            for d in (4, 3, 2, 1):
                low = WINDOW - d * rows
                sent[head, d - 1] = acc[:, low : low + rows, :].astype(sent.dtype)
                if d > 2:
                    @pl.when(me >= d)
                    def _():
                        back_copy(head, d).start()
            dkv_ref[head] = acc[:, WINDOW : WINDOW + rows, :]

        return carry

    lax.fori_loop(0, heads + 5, step, 0)

    def drain(head, carry):
        @pl.when((odd == 0) | (me >= 2))
        def _():
            kv_copy(head, 1).wait_send()

        @pl.when(me + 2 < n)
        def _():
            kv_copy(head, 2).wait_send()

            @pl.when(me >= 1)
            def _():
                kv_copy(head, 3).wait_send()

            @pl.when(me >= 2)
            def _():
                kv_copy(head, 4).wait_send()

        for d in range(1, hops + 1):
            @pl.when(me >= d)
            def _():
                back_copy(head, d).wait_send()
        return carry

    lax.fori_loop(0, heads, drain, 0)
    for d in range(1, hops + 1):
        @pl.when(me + d < n)
        def _():
            mark_copy(d).wait_send()
    for k in range(len(bits)):
        count_copy(k).wait_send()
    total_ref[...] = count[len(bits)]


def on_device(queries, keys, values, d_out, loss_mask, turn_ids):
    rows, heads_q, depth = queries.shape[1:]
    heads = keys.shape[2]
    group = heads_q // heads
    n = lax.axis_size("ctx")
    hops = WINDOW // rows
    strips = rows // STRIP
    wide = group * STRIP
    pairs = lax.axis_size("dp")
    rounds = n.bit_length() + pairs.bit_length() - 2
    count = jnp.full((8, 128), jnp.sum(loss_mask).astype(jnp.float32))

    def by_strip(array):
        array = array.reshape(strips, STRIP, heads, group, depth)
        return array.transpose(2, 0, 3, 1, 4).reshape(heads, strips, wide, depth)

    q = by_strip(queries[0])
    g = by_strip(d_out[0] * loss_mask[0][:, None, None].astype(jnp.bfloat16))
    kv = jnp.stack([keys[0], values[0]]).transpose(2, 0, 1, 3)
    turn = turn_ids[0]
    own_low = jnp.sum((turn[None, :] < turn[:, None]).astype(jnp.int32), axis=1)
    own_low = own_low.reshape(strips, 1, 1, STRIP)
    own_low = jnp.broadcast_to(own_low, (strips, 8, group, STRIP)).reshape(strips, 8, wide)
    mark = jnp.broadcast_to(turn[None, :], (8, rows))
    vmem = pl.BlockSpec(memory_space=pltpu.VMEM)
    span = WINDOW + rows
    dq, dkv, total = pl.pallas_call(
        functools.partial(kernel, n, pairs, rows),
        out_shape=(
            jax.ShapeDtypeStruct((heads, strips, wide, depth), jnp.float32),
            jax.ShapeDtypeStruct((heads, 2, rows, depth), jnp.float32),
            jax.ShapeDtypeStruct((8, 128), jnp.float32),
        ),
        in_specs=[vmem] * 6,
        out_specs=(vmem, vmem, vmem),
        scratch_shapes=[
            pltpu.VMEM((heads, 2, span, depth), jnp.bfloat16),
            pltpu.VMEM((heads, hops, 2, rows, depth), jnp.bfloat16),
            pltpu.VMEM((heads, hops, 2, rows, depth), jnp.bfloat16),
            pltpu.VMEM((hops, 8, rows), jnp.int32),
            pltpu.VMEM((strips, WINDOW + STRIP, wide), jnp.float32),
            pltpu.VMEM((2, span, depth), jnp.float32),
            pltpu.VMEM((rounds + 1, 8, 128), jnp.float32),
            pltpu.VMEM((rounds, 8, 128), jnp.float32),
            pltpu.SemaphoreType.DMA((hops,)),
            pltpu.SemaphoreType.DMA((hops,)),
            pltpu.SemaphoreType.DMA((heads, hops)),
            pltpu.SemaphoreType.DMA((heads, hops)),
            pltpu.SemaphoreType.DMA((heads, hops)),
            pltpu.SemaphoreType.DMA((heads, hops)),
            pltpu.SemaphoreType.DMA((rounds,)),
            pltpu.SemaphoreType.DMA((rounds,)),
        ],
        compiler_params=pltpu.CompilerParams(
            collective_id=0, has_side_effects=True, vmem_limit_bytes=56 << 20
        ),
    )(q, g, kv, mark, own_low, count)
    factor = rows * n * pairs / total[0, 0]
    d_q = (dq * (factor * SCALE)).astype(jnp.bfloat16)
    d_q = d_q.reshape(heads, strips, group, STRIP, depth).transpose(1, 3, 0, 2, 4)
    d_queries = d_q.reshape(1, rows, heads_q, depth)
    d_keys = (dkv[:, 0] * (factor * SCALE)).astype(jnp.bfloat16).transpose(1, 0, 2)[None]
    d_values = (dkv[:, 1] * factor).astype(jnp.bfloat16).transpose(1, 0, 2)[None]
    return (d_queries, d_keys, d_values)


def solution(mesh):
    spec = P("dp", "ctx", "head", None)
    return jax.shard_map(
        on_device,
        mesh=mesh,
        in_specs=(spec, spec, spec, spec, P("dp", "ctx"), P("dp", "ctx")),
        out_specs=(spec, spec, spec),
        check_vma=False,
    )
```

```python
import functools
import math

import jax
import jax.numpy as jnp
from jax import lax
from jax.experimental import pallas as pl
from jax.experimental.pallas import tpu as pltpu
from jax.sharding import PartitionSpec as P

WINDOW = 1024
SCALE = 168.0 ** (-0.5)
STRIP = 128
MASKED = -1e30
AHEAD = 2


def head_grads(head, rows, q_ref, g_ref, ext, bias, acc, dq_ref):
    span = WINDOW + STRIP
    for strip in range(rows // STRIP):
        low = strip * STRIP
        query = q_ref[head, strip]
        grad = g_ref[head, strip]
        key = ext[head, 0, low : low + span, :]
        value = ext[head, 1, low : low + span, :]
        logits = lax.dot_general(
            key, query, (((1,), (1,)), ((), ())), preferred_element_type=jnp.float32
        )
        logits = logits * (SCALE * math.log2(math.e)) + bias[strip]
        top = jnp.max(logits, axis=0, keepdims=True)
        raised = jnp.exp2(logits - top)
        prob = raised * (1.0 / jnp.sum(raised, axis=0, keepdims=True))
        grad_prob = lax.dot_general(
            value, grad, (((1,), (1,)), ((), ())), preferred_element_type=jnp.float32
        )
        delta = jnp.sum(prob * grad_prob, axis=0, keepdims=True)
        grad_logit = (prob * (grad_prob - delta)).astype(jnp.bfloat16)
        dq_ref[head, strip] = lax.dot_general(
            grad_logit, key, (((0,), (0,)), ((), ())), preferred_element_type=jnp.float32
        )
        parts = (
            jnp.dot(grad_logit, query, preferred_element_type=jnp.float32),
            jnp.dot(prob.astype(jnp.bfloat16), grad, preferred_element_type=jnp.float32),
        )
        for kind, part in enumerate(parts):
            if strip == 0:
                acc[kind, :span] = part
            else:
                cut = span - STRIP
                acc[kind, low : low + cut] += part[:cut]
                acc[kind, low + cut : low + span] = part[cut:]


def fill_bias(rows, mark_ref, marks, bias):
    hops = WINDOW // rows
    first = mark_ref[0:1, 0:1]
    before = jnp.zeros((1, 1), jnp.float32)
    for hop in range(hops):
        earlier = jnp.where(marks[hop, 0:1, :] < first, 1.0, 0.0)
        before += jnp.sum(earlier, axis=1, keepdims=True)
    for strip in range(rows // STRIP):
        turn = mark_ref[0:1, strip * STRIP : (strip + 1) * STRIP].astype(jnp.float32)
        own = jnp.zeros((1, STRIP), jnp.float32)
        for block in range(strip + 1):
            keys = mark_ref[0:1, block * STRIP : (block + 1) * STRIP].astype(jnp.float32)
            keys = jnp.transpose(jnp.broadcast_to(keys, (STRIP, STRIP)))
            own += jnp.sum(jnp.where(keys < turn, 1.0, 0.0), axis=0, keepdims=True)
        own = jnp.concatenate([own] * (bias.shape[2] // STRIP), axis=1)
        start = jnp.where(own > 0.0, own + WINDOW, before) - strip * STRIP
        shape = bias.shape[1:]
        row = lax.broadcasted_iota(jnp.int32, (1, shape[1]), 1) & (STRIP - 1)
        lowest = jnp.maximum(start.astype(jnp.int32), row + 1)
        col = lax.broadcasted_iota(jnp.int32, shape, 0)
        ok = (col >= lowest) & (col <= row + WINDOW)
        bias[strip] = jnp.where(ok, 0.0, MASKED)


def kernel(
    n, pairs, rows, q_ref, g_ref, kv_ref, turn_ref, mask_ref,
    dq_ref, dkv_ref,
    ext, own, dq_raw, mark_ref, sent, back, marks, bias, acc, count, count_in,
    mark_send, mark_recv, kv_send, kv_recv, back_send, back_recv, count_send, count_recv,
):
    hops = WINDOW // rows
    heads = kv_ref.shape[0]
    me = lax.axis_index("ctx")
    odd = me % 2
    other = me + 1 - 2 * odd
    bits = [("ctx", 1 << b) for b in range(n.bit_length() - 1)]
    bits += [("dp", 1 << b) for b in range(pairs.bit_length() - 1)]

    def remote(src, dst, send, recv, device):
        return pltpu.make_async_remote_copy(
            src_ref=src, dst_ref=dst, send_sem=send, recv_sem=recv,
            device_id=device, device_id_type=pl.DeviceIdType.MESH,
        )

    def partner(axis, bit):
        at = lax.axis_index(axis)
        return {axis: at + bit - 2 * bit * ((at // bit) % 2)}

    def mark_copy(d):
        return remote(mark_ref, marks.at[d - 1], mark_send.at[d - 1], mark_recv.at[d - 1],
                      {"ctx": me + d})

    def count_copy(k):
        return remote(count.at[k], count_in.at[k], count_send.at[k], count_recv.at[k],
                      partner(*bits[k]))

    def slot(head, d):
        return ext.at[head, :, pl.ds(WINDOW - d * rows, rows), :]

    def kv_copy(head, d):
        if d == 1:
            return remote(slot(head, 2), slot(head, 1), kv_send.at[head, 0],
                          kv_recv.at[head, 0], {"ctx": other})
        src = kv_ref.at[head] if d == 2 else slot(head, d - 2)
        return remote(src, slot(head, d), kv_send.at[head, d - 1], kv_recv.at[head, d - 1],
                      {"ctx": me + 2})

    def own_across(head):
        return remote(kv_ref.at[head], slot(head, 1), kv_send.at[head, 0],
                      kv_recv.at[head, 0], {"ctx": other})

    def back_copy(head, d):
        return remote(sent.at[head, d - 1], back.at[head, d - 1], back_send.at[head, d - 1],
                      back_recv.at[head, d - 1], {"ctx": other if d == 1 else me - 2})

    def add_in(head, d, taken):
        sent[head, d - 1] = (
            sent[head, d - 1].astype(jnp.float32) + back[head, taken - 1].astype(jnp.float32)
        ).astype(sent.dtype)

    barrier = pltpu.get_barrier_semaphore()

    def greet(device):
        pl.semaphore_signal(barrier, inc=1, device_id=device,
                            device_id_type=pl.DeviceIdType.MESH)

    for d in range(1, hops + 1):
        @pl.when(me + d < n)
        def _():
            greet({"ctx": me + d})

        @pl.when(me >= d)
        def _():
            greet({"ctx": me - d})
    far = [b for b in bits if b[0] == "dp" or b[1] > hops]
    for b in far:
        greet(partner(*b))
    pl.semaphore_wait(
        barrier, jnp.minimum(me, hops) + jnp.minimum(n - 1 - me, hops) + len(far)
    )

    def send_own(head):
        @pl.when(me + 2 < n)
        def _():
            kv_copy(head, 2).start()

        @pl.when(odd == 0)
        def _():
            own_across(head).start()

    mark_ref[...] = jnp.broadcast_to(turn_ref[...], mark_ref.shape)
    for d in range(1, hops + 1):
        @pl.when(me + d < n)
        def _():
            mark_copy(d).start()
    for head in range(min(AHEAD, heads)):
        send_own(head)
    ones = jnp.sum(mask_ref[...].astype(jnp.float32), axis=1, keepdims=True)
    count[0] = jnp.broadcast_to(ones, count.shape[1:])
    count_copy(0).start()

    def place_own(head, carry):
        ext[head, :, WINDOW : WINDOW + rows, :] = kv_ref[head]
        for d in range(1, hops + 1):
            @pl.when(me < d)
            def _():
                ext[head, :, WINDOW - d * rows : WINDOW - (d - 1) * rows, :] = jnp.zeros(
                    (2, rows, kv_ref.shape[3]), kv_ref.dtype
                )
        return carry

    lax.fori_loop(0, heads, place_own, 0)

    for d in range(1, hops + 1):
        @pl.when(me < d)
        def _():
            marks[d - 1] = jnp.full(mark_ref.shape, -1, jnp.int32)

        @pl.when(me >= d)
        def _():
            mark_copy(d).wait_recv()
    fill_bias(rows, mark_ref, marks, bias)

    def step(s, carry):
        for k in range(len(bits)):
            @pl.when(s == k // 2)
            def _():
                count_copy(k).wait_recv()
                count[k + 1] = count[k] + count_in[k]
                if k + 1 < len(bits):
                    count_copy(k + 1).start()

        @pl.when(s + AHEAD < heads)
        def _():
            send_own(s + AHEAD)

        @pl.when(s < heads)
        def _():
            @pl.when(me >= 2)
            def _():
                kv_copy(s, 2).wait_recv()

                @pl.when(odd == 1)
                def _():
                    kv_copy(s, 1).start()

                @pl.when(me + 2 < n)
                def _():
                    kv_copy(s, 4).start()

            @pl.when(odd == 1)
            def _():
                kv_copy(s, 1).wait_recv()

                @pl.when(me + 2 < n)
                def _():
                    kv_copy(s, 3).start()

        @pl.when((s >= 1) & (s < heads + 1) & (odd == 0) & (me >= 2))
        def _():
            kv_copy(s - 1, 1).wait_recv()

            @pl.when(me + 2 < n)
            def _():
                kv_copy(s - 1, 3).start()

        @pl.when((s >= 2) & (s < heads + 2))
        def _():
            head = s - 2
            for d in (3, 4):
                @pl.when(me >= d)
                def _():
                    kv_copy(head, d).wait_recv()
            head_grads(head, rows, q_ref, g_ref, ext, bias, acc, dq_raw)
            for d in (3, 4, 2, 1):
                low = WINDOW - d * rows
                sent[head, d - 1] = acc[:, low : low + rows, :].astype(sent.dtype)
                if d > 2:
                    @pl.when(me >= d)
                    def _():
                        back_copy(head, d).start()
            own[head] = acc[:, WINDOW : WINDOW + rows, :]

        @pl.when((s >= 3) & (s < heads + 3))
        def _():
            head = s - 3

            @pl.when(me >= 1)
            def _():
                @pl.when(me + 2 < n)
                def _():
                    back_copy(head, 3).wait_recv()
                    add_in(head, 1, 3)

                back_copy(head, 1).start()

            @pl.when((odd == 0) & (me >= 2))
            def _():
                @pl.when(me + 2 < n)
                def _():
                    back_copy(head, 4).wait_recv()
                    add_in(head, 2, 4)

                back_copy(head, 2).start()

        @pl.when((s >= 4) & (s < heads + 4) & (odd == 1) & (me >= 2))
        def _():
            head = s - 4

            @pl.when(me + 2 < n)
            def _():
                back_copy(head, 4).wait_recv()
                add_in(head, 2, 4)

            back_copy(head, 1).wait_recv()
            add_in(head, 2, 1)
            back_copy(head, 2).start()

        @pl.when(s >= 5)
        def _():
            head = s - 5

            @pl.when(odd == 0)
            def _():
                back_copy(head, 1).wait_recv()
                own[head] += back[head, 0].astype(jnp.float32)

            @pl.when(me + 2 < n)
            def _():
                back_copy(head, 2).wait_recv()
                own[head] += back[head, 1].astype(jnp.float32)

            factor = (rows * n * pairs) / count[len(bits), 0:1, 0:1]
            dkv_ref[head, 0] = (own[head, 0] * (factor * SCALE)).astype(dkv_ref.dtype)
            dkv_ref[head, 1] = (own[head, 1] * factor).astype(dkv_ref.dtype)
            for strip in range(rows // STRIP):
                dq_ref[head, strip] = (
                    dq_raw[head, strip] * (factor * SCALE)
                ).astype(dq_ref.dtype)

        return carry

    lax.fori_loop(0, heads + 5, step, 0)

    def drain(head, carry):
        @pl.when((odd == 0) | (me >= 2))
        def _():
            kv_copy(head, 1).wait_send()

        @pl.when(me + 2 < n)
        def _():
            kv_copy(head, 2).wait_send()

            @pl.when(me >= 1)
            def _():
                kv_copy(head, 3).wait_send()

            @pl.when(me >= 2)
            def _():
                kv_copy(head, 4).wait_send()

        for d in range(1, hops + 1):
            @pl.when(me >= d)
            def _():
                back_copy(head, d).wait_send()
        return carry

    lax.fori_loop(0, heads, drain, 0)
    for d in range(1, hops + 1):
        @pl.when(me + d < n)
        def _():
            mark_copy(d).wait_send()
    for k in range(len(bits)):
        count_copy(k).wait_send()


def on_device(queries, keys, values, d_out, loss_mask, turn_ids):
    rows, heads_q, depth = queries.shape[1:]
    heads = keys.shape[2]
    group = heads_q // heads
    n = lax.axis_size("ctx")
    hops = WINDOW // rows
    strips = rows // STRIP
    wide = group * STRIP
    pairs = lax.axis_size("dp")
    rounds = n.bit_length() + pairs.bit_length() - 2

    def by_strip(array):
        array = array.reshape(strips, STRIP, heads, group, depth)
        return array.transpose(2, 0, 3, 1, 4).reshape(heads, strips, wide, depth)

    q = by_strip(queries[0])
    g = by_strip(d_out[0] * loss_mask[0][:, None, None].astype(jnp.bfloat16))
    kv = jnp.stack([keys[0], values[0]]).transpose(2, 0, 1, 3)
    vmem = pl.BlockSpec(memory_space=pltpu.VMEM)
    span = WINDOW + rows
    dq, dkv = pl.pallas_call(
        functools.partial(kernel, n, pairs, rows),
        out_shape=(
            jax.ShapeDtypeStruct((heads, strips, wide, depth), jnp.bfloat16),
            jax.ShapeDtypeStruct((heads, 2, rows, depth), jnp.bfloat16),
        ),
        in_specs=[vmem] * 5,
        out_specs=(vmem, vmem),
        scratch_shapes=[
            pltpu.VMEM((heads, 2, span, depth), jnp.bfloat16),
            pltpu.VMEM((heads, 2, rows, depth), jnp.float32),
            pltpu.VMEM((heads, strips, wide, depth), jnp.float32),
            pltpu.VMEM((8, rows), jnp.int32),
            pltpu.VMEM((heads, hops, 2, rows, depth), jnp.bfloat16),
            pltpu.VMEM((heads, hops, 2, rows, depth), jnp.bfloat16),
            pltpu.VMEM((hops, 8, rows), jnp.int32),
            pltpu.VMEM((strips, WINDOW + STRIP, wide), jnp.float32),
            pltpu.VMEM((2, span, depth), jnp.float32),
            pltpu.VMEM((rounds + 1, 8, 128), jnp.float32),
            pltpu.VMEM((rounds, 8, 128), jnp.float32),
            pltpu.SemaphoreType.DMA((hops,)),
            pltpu.SemaphoreType.DMA((hops,)),
            pltpu.SemaphoreType.DMA((heads, hops)),
            pltpu.SemaphoreType.DMA((heads, hops)),
            pltpu.SemaphoreType.DMA((heads, hops)),
            pltpu.SemaphoreType.DMA((heads, hops)),
            pltpu.SemaphoreType.DMA((rounds,)),
            pltpu.SemaphoreType.DMA((rounds,)),
        ],
        compiler_params=pltpu.CompilerParams(
            collective_id=0, has_side_effects=True, vmem_limit_bytes=56 << 20
        ),
    )(q, g, kv, turn_ids, loss_mask)
    dq = dq.reshape(heads, strips, group, STRIP, depth).transpose(1, 3, 0, 2, 4)
    d_queries = dq.reshape(1, rows, heads_q, depth)
    d_keys = dkv[:, 0].transpose(1, 0, 2)[None]
    d_values = dkv[:, 1].transpose(1, 0, 2)[None]
    return (d_queries, d_keys, d_values)


def solution(mesh):
    spec = P("dp", "ctx", "head", None)
    return jax.shard_map(
        on_device,
        mesh=mesh,
        in_specs=(spec, spec, spec, spec, P("dp", "ctx"), P("dp", "ctx")),
        out_specs=(spec, spec, spec),
        check_vma=False,
    )
```
